256 devices in a mesh: tensor: 4 (over x_hi, core), context: 64 (over x_lo, y, z).
Axes of the slice: x: 4 (x_hi: 2, x_lo: 2; x = x_hi * 2 + x_lo), y: 4, z: 8, core: 2. Of those that a mesh axis runs over, the one named last changes fastest.
Arguments:
- query_states: bfloat16 [16384, 512], P('context', 'tensor'), may hold values from -6 to 6
- key_states: bfloat16 [16384, 512], P('context', 'tensor'), may hold values from -6 to 6
- value_states: bfloat16 [16384, 512], P('context', 'tensor'), may hold values from -6 to 6
- out_grad: bfloat16 [16384, 6144], P('context', 'tensor'), may hold values from -16 to 16
- out_proj: bfloat16 [6144, 512], P(None, 'tensor'), may hold values from -0.25 to 0.25
Outputs:
- query_grad: bfloat16 [16384, 512], P('context', 'tensor')
- key_grad: bfloat16 [16384, 512], P('context', 'tensor')
- value_grad: bfloat16 [16384, 512], P('context', 'tensor')
- proj_grad: float32 [6144, 512], P('context', 'tensor')
The draws below stay inside these ranges and needn't reach their ends.
All inputs are finite; a program needn't handle non-finite values.
Results may differ from the reference program's by a relative error of at most 0.038.
Values may be sent and summed in bfloat16 or wider, within the bound.
A program may use at most 128 MiB of HBM per device.

```python
import math
import jax
import jax.numpy as jnp
from jax import lax

D = 6144
HD = 128
HEADS = 4
TOKENS = 16384


def draw_query_states(key, part):
    columns = HEADS * HD
    values = jnp.clip(1.2 * jax.random.normal(jax.random.fold_in(key, 11), (TOKENS, columns), jnp.float32), -6.0, 6.0)
    return values.astype(jnp.bfloat16)


def draw_key_states(key, part):
    columns = HEADS * HD
    values = jnp.clip(1.2 * jax.random.normal(jax.random.fold_in(key, 12), (TOKENS, columns), jnp.float32), -6.0, 6.0)
    return values.astype(jnp.bfloat16)


def strengthened(array, key, source, target, parts, factor):
    owner, partner = [(jnp.arange(array.shape[position]) // (array.shape[position] // parts)).reshape([-1 if axis == position else 1 for axis in range(array.ndim)]) for position in (source, target)]
    chosen = jax.random.permutation(key, parts)[partner]
    strong = (owner == chosen) | (owner == (partner + parts // 2) % parts)
    return jnp.where(strong, factor * array, array)


def block_scale(stream_key, shape, pieces, smallest, largest):
    level = 1.0
    for dim, blocks in pieces:
        heights = jax.random.uniform(jax.random.fold_in(jax.random.fold_in(stream_key, 6), dim), (blocks,), jnp.float32, smallest / len(pieces), largest / len(pieces))
        level = level * jnp.repeat(jnp.exp(heights), shape[dim] // blocks).reshape((-1,) + (1,) * (len(shape) - 1 - dim))
    return level


def bell_draw(own_key, extent, scale, reach, pieces=(), dtype=jnp.bfloat16):
    values = scale * jax.random.normal(own_key, extent, jnp.float32)
    if pieces:
        values = values * block_scale(own_key, extent, pieces, -0.22, 0.18)
    return jnp.clip(values, -reach, reach).astype(dtype)


def gaussian_with(own_key, shape, scale, most, shards, heavy, dtype=jnp.bfloat16):
    drawn = scale * jax.random.normal(own_key, shape, jnp.float32)
    if shards:
        drawn = drawn * block_scale(own_key, shape, shards, -0.22, 0.18)
    return jnp.clip(strengthened(drawn, jax.random.fold_in(own_key, 3), *heavy), -most, most).astype(dtype)


def setup_inputs(seed: int = 0) -> dict:
    arg_keys = jax.random.split(jax.random.key(seed), 6)
    return {
        "query_states": draw_query_states(jax.random.fold_in(arg_keys[5], 71), 0),
        "key_states": draw_key_states(jax.random.fold_in(arg_keys[5], 71), 0),
        "value_states": bell_draw(arg_keys[2], (TOKENS, HEADS * HD), 1.0, 6.0, ((0, 64), (1, 4))),
        "out_grad": gaussian_with(arg_keys[3], (TOKENS, D), 1.0, 16.0, ((0, 64), (1, 4)), (0, 1, 64, 4.0)),
        "out_proj": bell_draw(arg_keys[4], (D, HEADS * HD), (HEADS * HD) ** -0.5, 0.25, ((1, 4),)),
    }


log_two_e = 1.4426950408889634


def reference(query_states, key_states, value_states, out_grad, out_proj):
    scaling = HD ** -0.5
    score_scale = scaling * log_two_e
    block_rows = math.gcd(TOKENS, 1024)
    block_count = TOKENS // block_rows
    attended_grad = jnp.dot(out_grad, out_proj, preferred_element_type=jnp.float32).astype(jnp.bfloat16)
    attended_parts = []
    query_parts = []
    key_parts = []
    value_parts = []
    for head_index in range(HEADS):
        first_column = head_index * HD
        query_head = query_states[:, first_column:first_column + HD]
        key_head = key_states[:, first_column:first_column + HD]
        value_head = value_states[:, first_column:first_column + HD]
        grad_head = attended_grad[:, first_column:first_column + HD]

        def forward_rows(query_block, key_head=key_head, value_head=value_head):
            scores = jnp.dot(query_block, key_head.T, preferred_element_type=jnp.float32) * score_scale
            row_shift = jnp.ceil(jnp.max(scores, axis=1))
            powers = jnp.exp2(scores - row_shift[:, None])
            row_total = jnp.sum(powers, axis=1)
            weighted = jnp.dot(powers.astype(jnp.bfloat16), value_head, preferred_element_type=jnp.float32)
            return (weighted / row_total[:, None]).astype(jnp.bfloat16), row_shift + jnp.log2(row_total)

        attended_head, log_total = lax.map(forward_rows, query_head.reshape(block_count, block_rows, HD))
        attended_head = attended_head.reshape(TOKENS, HD)
        log_total = log_total.reshape(TOKENS)
        row_delta = jnp.sum(attended_head.astype(jnp.float32) * grad_head.astype(jnp.float32), axis=1)

        def backward_rows(running, inputs, key_head=key_head, value_head=value_head):
            query_block, grad_block, total_block, delta_block = inputs
            scores = jnp.dot(query_block, key_head.T, preferred_element_type=jnp.float32) * score_scale
            weights = jnp.exp2(scores - total_block[:, None])
            prob_grad = jnp.dot(grad_block, value_head.T, preferred_element_type=jnp.float32)
            score_grad = (weights * (prob_grad - delta_block[:, None])).astype(jnp.bfloat16)
            block_grad = (jnp.dot(score_grad, key_head, preferred_element_type=jnp.float32) * scaling).astype(jnp.bfloat16)
            key_sum = running[0] + jnp.dot(score_grad.T, query_block, preferred_element_type=jnp.float32)
            value_sum = running[1] + jnp.dot(weights.astype(jnp.bfloat16).T, grad_block, preferred_element_type=jnp.float32)
            return (key_sum, value_sum), block_grad

        empty_sum = jnp.zeros((TOKENS, HD), jnp.float32)
        sequences = (query_head.reshape(block_count, block_rows, HD), grad_head.reshape(block_count, block_rows, HD),
                     log_total.reshape(block_count, block_rows), row_delta.reshape(block_count, block_rows))
        (key_sum, value_sum), query_head_grad = lax.scan(backward_rows, (empty_sum, empty_sum), sequences)
        attended_parts.append(attended_head)
        query_parts.append(query_head_grad.reshape(TOKENS, HD))
        key_parts.append((key_sum * scaling).astype(jnp.bfloat16))
        value_parts.append(value_sum.astype(jnp.bfloat16))
    attended = jnp.concatenate(attended_parts, axis=1)
    proj_grad = jnp.dot(out_grad.T, attended, preferred_element_type=jnp.float32)
    return (jnp.concatenate(query_parts, axis=1), jnp.concatenate(key_parts, axis=1),
            jnp.concatenate(value_parts, axis=1), proj_grad)
```

```python
import jax
import jax.numpy as jnp
from jax import lax
from jax.experimental import pallas as pl
from jax.experimental.pallas import tpu as pltpu
from jax.sharding import Mesh
from jax.sharding import PartitionSpec as P

HD = 128
ROWS = 256
TENSOR = ("tensor_0", "tensor_1")
CONTEXT = ("context_0", "context_1", "context_2")
SCALING = HD ** (-0.5)
SCORE_SCALE = SCALING * 1.4426950408889634
FEATURES = 1536
HALF = FEATURES // 2
PIECE = HALF // 8

BF16 = jnp.bfloat16
F32 = jnp.float32

(Q, K, V, G, O, L, ST, DQ, DK, DV, W, PA, A, S1, S2) = range(15)


def dot(a, b, ca, cb):
    return lax.dot_general(a, b, (((ca,), (cb,)), ((), ())), preferred_element_type=F32)


def fold(x, op):
    return op(x.reshape(x.shape[0] // 8, 8, x.shape[1]), axis=0)


def z_offset(i):
    odd = lax.rem(i, 2)
    return odd * lax.div(i + 1, 2) + (1 - odd) * lax.rem(8 - lax.div(i, 2), 8)


def kernel(
    q_in, k_in, v_in, og_in, w_in,
    dq_out, dk_out, dv_out, dw_out,
    qg, kg, vg, kt, vt, og, ogt, wg, part, part_in, gt, gs,
    s_tile, powers, grads, shift,
    o_send, o_in, l_send, l_in, st_send, st_in,
    att, dq_send, dq_in, dk_send, dk_in, dv_send, dv_in,
    s1_send, s1_in, s2_send, s2_in,
    send, recv, here,
):
    xh = lax.axis_index("tensor_0")
    co = lax.axis_index("tensor_1")
    xl = lax.axis_index("context_0")
    y = lax.axis_index("context_1")
    z = lax.axis_index("context_2")

    def z_to(i):
        return {"context_2": lax.rem(z + z_offset(i), 8)}

    def z_back(i):
        return {"context_2": lax.rem(z + 8 - z_offset(i), 8)}

    def u_to(e):
        return {
            "context_0": lax.rem(xl + lax.div(e, 4), 2),
            "context_1": lax.rem(y + lax.rem(e, 4), 4),
        }

    def u_back(e):
        return {
            "context_0": lax.rem(xl + lax.div(e, 4), 2),
            "context_1": lax.rem(y + 4 - lax.rem(e, 4), 4),
        }

    def t_to(s):
        return {
            "tensor_0": lax.rem(xh + s // 2, 2),
            "tensor_1": lax.rem(co + s % 2, 2),
        }

    def w_to(s):
        target = t_to(s)
        if s // 2:
            target["context_0"] = 1 - xl
        return target

    t_is_u = jnp.logical_and(xl == xh, lax.div(y, 2) == co)

    def s2_to(i):
        return {
            "tensor_0": xl,
            "tensor_1": lax.div(y, 2),
            "context_0": xh,
            "context_1": 2 * co + lax.rem(y, 2),
            "context_2": lax.rem(z + z_offset(i), 8),
        }

    def remote(src, dst, row, slot, target):
        return pltpu.make_async_remote_copy(
            src_ref=src,
            dst_ref=dst,
            send_sem=send.at[row, slot],
            recv_sem=recv.at[row, slot],
            device_id=target,
            device_id_type=pl.DeviceIdType.MESH,
        )

    def rows(ref, e, count=ROWS):
        return ref.at[pl.ds(e * count, count)]

    tensor_place = 2 * xh + co
    local = [
        pltpu.make_async_copy(q_in, rows(qg, 0), here.at[0]),
        pltpu.make_async_copy(k_in, rows(kg, 0), here.at[1]),
        pltpu.make_async_copy(v_in, rows(vg, 0), here.at[2]),
        pltpu.make_async_copy(og_in, og, here.at[3]),
        pltpu.make_async_copy(
            w_in.at[pl.ds(pl.multiple_of(tensor_place * FEATURES, FEATURES), FEATURES)],
            wg.at[0],
            here.at[4],
        ),
    ]
    for copy in local:
        copy.start()

    barrier = pltpu.get_barrier_semaphore()

    def greet(target):
        pl.semaphore_signal(
            barrier, inc=1, device_id=target, device_id_type=pl.DeviceIdType.MESH
        )

    for i in range(1, 8):
        greet(z_to(i))
        greet(u_to(i))
        greet(s2_to(i))
    for s in range(1, 4):
        greet(t_to(s))
    for s in range(2, 4):
        greet(w_to(s))

    @pl.when(jnp.logical_not(t_is_u))
    def _():
        greet(s2_to(0))
        pl.semaphore_wait(barrier, 27)

    @pl.when(t_is_u)
    def _():
        pl.semaphore_wait(barrier, 26)

    def q_copy(i):
        return remote(q_in, rows(qg, i), Q, i, z_to(i))

    def k_copy(e):
        return remote(k_in, rows(kg, e), K, e, u_to(e))

    def v_copy(e):
        return remote(v_in, rows(vg, e), V, e, u_to(e))

    def w_copy(s):
        place = 2 * lax.rem(xh + s // 2, 2) + lax.rem(co + s % 2, 2)
        block = w_in.at[pl.ds(pl.multiple_of(place * FEATURES, FEATURES), FEATURES)]
        return remote(block, wg.at[s], W, s, w_to(s))

    near = (1, 3, 4, 5, 7, 2, 6)
    for i, e in enumerate(near):
        k_copy(e).start()
        q_copy(i + 1).start()
    for s in (1, 2, 3):
        w_copy(s).start()
    for e in near:
        v_copy(e).start()
    for copy in local:
        copy.wait()

    for c in range(FEATURES // ROWS):
        ogt[c * ROWS : (c + 1) * ROWS, :] = (
            og[:, c * ROWS : (c + 1) * ROWS].astype(F32).T.astype(BF16)
        )

    for e in (0,) + near:
        if e:
            k_copy(e).wait_recv()
        kt[:, e * ROWS : (e + 1) * ROWS] = kg[e * ROWS : (e + 1) * ROWS, :].astype(F32).T.astype(BF16)
    for e in (0,) + near:
        if e:
            v_copy(e).wait_recv()
        vt[:, e * ROWS : (e + 1) * ROWS] = vg[e * ROWS : (e + 1) * ROWS, :].astype(F32).T.astype(BF16)

    def o_copy(i):
        return remote(o_send.at[i], o_in.at[i], O, i, z_back(i))

    def l_copy(i):
        return remote(l_send.at[i], l_in.at[i], L, i, z_back(i))

    def forward(i, unused):
        @pl.when(i > 0)
        def _():
            q_copy(i).wait_recv()

        lanes = pl.ds(pl.multiple_of(i * ROWS, ROWS), ROWS)
        q_block = qg[lanes, :]
        top = None
        for j in range(8):
            part_rows = slice(j * ROWS, (j + 1) * ROWS)
            scores = dot(kg[part_rows, :], q_block, 1, 1) * SCORE_SCALE
            s_tile[part_rows, :] = scores
            highest = fold(scores, jnp.max)
            top = highest if top is None else jnp.maximum(top, highest)
        row_shift = jnp.ceil(jnp.max(top, axis=0, keepdims=True))
        shift[i] = row_shift
        total = jnp.zeros((8, ROWS), F32)
        weighted = jnp.zeros((HD, ROWS), F32)
        for j in range(8):
            part_rows = slice(j * ROWS, (j + 1) * ROWS)
            p = jnp.exp2(s_tile[part_rows, :] - row_shift)
            total = total + fold(p, jnp.sum)
            p = p.astype(BF16)
            powers[part_rows, lanes] = p
            weighted = weighted + dot(vt[:, part_rows], p, 1, 0)
        row_total = jnp.sum(total, axis=0, keepdims=True)
        o_send[i] = (weighted / row_total).astype(BF16)
        l_send[i] = jnp.broadcast_to(row_shift + jnp.log2(row_total), (8, ROWS))

        @pl.when(i > 0)
        def _():
            o_copy(i).start()
            l_copy(i).start()

        return unused

    lax.fori_loop(0, 8, forward, 0)

    def part_copy(s):
        return remote(part.at[s], part_in.at[s], PA, s, t_to(s))

    for s in (2, 3, 1):
        w_copy(s).wait_recv()
        part[s] = dot(og[...], wg[s], 1, 0).astype(BF16)
        part_copy(s).start()
    g_sum = dot(og[...], wg[0], 1, 0)
    for s in (1, 2, 3):
        part_copy(s).wait_recv()
        g_sum = g_sum + part_in[s].astype(F32)
    g_own = g_sum.T.astype(BF16)
    gt[0] = g_own

    def g_copy(i):
        return remote(gt.at[0], gt.at[i], G, i, z_to(i))

    for i in range(1, 8):
        g_copy(i).start()

    for i in range(1, 8):
        l_copy(i).wait_recv()
    log_parts = [l_send[0][0:1, :]] + [l_in[i][0:1, :] for i in range(1, 8)]
    highest = log_parts[0]
    for value in log_parts[1:]:
        highest = jnp.maximum(highest, value)
    factors = [jnp.exp2(value - highest) for value in log_parts]
    total = factors[0]
    for value in factors[1:]:
        total = total + value
    joined = (factors[0] / total) * o_send[0].astype(F32)
    for i in range(1, 8):
        o_copy(i).wait_recv()
        joined = joined + (factors[i] / total) * o_in[i].astype(F32)
    attended = joined.astype(BF16)
    att[0] = attended

    def a_copy(s):
        return remote(att.at[0], att.at[s], A, s, t_to(s))

    for s in (2, 3, 1):
        a_copy(s).start()

    log_total = highest + jnp.log2(total)
    row_delta = jnp.sum(attended.astype(F32) * g_own.astype(F32), axis=0, keepdims=True)
    st_send[0:8, :] = jnp.broadcast_to(log_total, (8, ROWS))
    st_send[8:16, :] = jnp.broadcast_to(row_delta, (8, ROWS))
    st_in[0] = st_send[...]

    def st_copy(i):
        return remote(st_send, st_in.at[i], ST, i, z_to(i))

    for i in range(1, 8):
        st_copy(i).start()

    def s1_copy(e):
        return remote(s1_send.at[e], s1_in.at[e], S1, e, u_to(e))

    for s in (1, 2, 3):
        a_copy(s).wait_recv()

    def project(e, unused):
        u = u_to(e)
        head_hi, head_lo = u["context_0"], lax.div(u["context_1"], 2)
        half = lax.rem(u["context_1"], 2)
        place = 2 * lax.rem(head_hi + xh, 2) + lax.rem(head_lo + co, 2)
        block = ogt[pl.ds(pl.multiple_of(half * HALF, HALF), HALF), :]
        s1_send[e] = dot(block, att[place], 1, 1).astype(BF16)

        @pl.when(e > 0)
        def _():
            s1_copy(e).start()

        return unused

    lax.fori_loop(0, 8, project, 0)

    def dq_copy(i):
        return remote(dq_send.at[i], dq_in.at[i], DQ, i, z_back(i))

    def backward(i, unused):
        @pl.when(i > 0)
        def _():
            g_copy(i).wait_recv()
            st_copy(i).wait_recv()

        lanes = pl.ds(pl.multiple_of(i * ROWS, ROWS), ROWS)
        factor = jnp.exp2(shift[i] - st_in[i, 0:1, :])
        delta = factor * st_in[i, 8:9, :]
        g_block = (gt[i].astype(F32) * factor).astype(BF16)
        gs[:, lanes] = g_block
        query_sum = jnp.zeros((HD, ROWS), F32)
        for j in range(8):
            part_rows = slice(j * ROWS, (j + 1) * ROWS)
            prob = dot(vg[part_rows, :], g_block, 1, 0)
            score = ((prob - delta) * powers[part_rows, lanes].astype(F32)).astype(BF16)
            grads[part_rows, lanes] = score
            query_sum = query_sum + dot(kt[:, part_rows], score, 1, 0)
        dq_send[i] = query_sum.astype(BF16)

        @pl.when(i > 0)
        def _():
            dq_copy(i).start()

        return unused

    lax.fori_loop(0, 8, backward, 0)

    def dk_copy(e):
        return remote(dk_send.at[e], dk_in.at[e], DK, e, u_back(e))

    def dv_copy(e):
        return remote(dv_send.at[e], dv_in.at[e], DV, e, u_back(e))

    def key_side(n, unused):
        e = lax.rem(n + 1, 8)
        part_rows = pl.ds(pl.multiple_of(e * ROWS, ROWS), ROWS)
        dk_send[e] = dot(grads[part_rows, :], qg[...], 1, 0).astype(BF16)

        @pl.when(e > 0)
        def _():
            dk_copy(e).start()

        dv_send[e] = dot(powers[part_rows, :], gs[...], 1, 1).astype(BF16)

        @pl.when(e > 0)
        def _():
            dv_copy(e).start()

        return unused

    lax.fori_loop(0, 8, key_side, 0)

    for e in range(1, 8):
        s1_copy(e).wait_recv()
    for c in range(8):
        piece = slice(c * PIECE, (c + 1) * PIECE)
        acc = s1_send[0, piece, :].astype(F32)
        for e in range(1, 8):
            acc = acc + s1_in[e, piece, :].astype(F32)
        s2_send[c] = acc.astype(BF16)

    def s2_copy(i):
        return remote(
            s2_send.at[lax.rem(z + z_offset(i), 8)], s2_in.at[i], S2, i, s2_to(i)
        )

    for i in range(1, 8):
        s2_copy(i).start()

    @pl.when(jnp.logical_not(t_is_u))
    def _():
        s2_copy(0).start()

    @pl.when(t_is_u)
    def _():
        s2_in[0] = s2_send[z]

    acc = dq_send[0].astype(F32)
    for i in range(1, 8):
        dq_copy(i).wait_recv()
        acc = acc + dq_in[i].astype(F32)
    dq_out[...] = (acc * SCALING).T.astype(BF16)
    acc = dk_send[0].astype(F32)
    for e in range(1, 8):
        dk_copy(e).wait_recv()
        acc = acc + dk_in[e].astype(F32)
    dk_out[...] = (acc * SCALING).astype(BF16)
    acc = dv_send[0].astype(F32)
    for e in range(1, 8):
        dv_copy(e).wait_recv()
        acc = acc + dv_in[e].astype(F32)
    dv_out[...] = acc.astype(BF16)

    @pl.when(jnp.logical_not(t_is_u))
    def _():
        s2_copy(0).wait_recv()

    acc = s2_in[0].astype(F32)
    for i in range(1, 8):
        s2_copy(i).wait_recv()
        acc = acc + s2_in[i].astype(F32)
    dw_out[...] = acc

    for i in range(1, 8):
        for copy in (q_copy, k_copy, v_copy, g_copy, o_copy, l_copy, st_copy, dq_copy, dk_copy,
                     dv_copy, s1_copy, s2_copy):
            copy(i).wait_send()
    for s in range(1, 4):
        for copy in (w_copy, part_copy, a_copy):
            copy(s).wait_send()

    @pl.when(jnp.logical_not(t_is_u))
    def _():
        s2_copy(0).wait_send()


def local(q, k, v, og, w):
    anywhere = pl.BlockSpec(memory_space=pl.ANY)
    vmem = pl.BlockSpec(memory_space=pltpu.VMEM)
    tokens = 8 * ROWS
    block = (8, ROWS, HD)
    turned = (8, HD, ROWS)
    return pl.pallas_call(
        kernel,
        out_shape=(
            jax.ShapeDtypeStruct((ROWS, HD), BF16),
            jax.ShapeDtypeStruct((ROWS, HD), BF16),
            jax.ShapeDtypeStruct((ROWS, HD), BF16),
            jax.ShapeDtypeStruct((PIECE, HD), F32),
        ),
        in_specs=[anywhere] * 5,
        out_specs=(vmem,) * 4,
        scratch_shapes=[
            pltpu.VMEM((tokens, HD), BF16),
            pltpu.VMEM((tokens, HD), BF16),
            pltpu.VMEM((tokens, HD), BF16),
            pltpu.VMEM((HD, tokens), BF16),
            pltpu.VMEM((HD, tokens), BF16),
            pltpu.VMEM((ROWS, FEATURES), BF16),
            pltpu.VMEM((FEATURES, ROWS), BF16),
            pltpu.VMEM((4, FEATURES, HD), BF16),
            pltpu.VMEM((4, ROWS, HD), BF16),
            pltpu.VMEM((4, ROWS, HD), BF16),
            pltpu.VMEM(turned, BF16),
            pltpu.VMEM((HD, tokens), BF16),
            pltpu.VMEM((tokens, ROWS), F32),
            pltpu.VMEM((tokens, tokens), BF16),
            pltpu.VMEM((tokens, tokens), BF16),
            pltpu.VMEM((8, 1, ROWS), F32),
            pltpu.VMEM(turned, BF16),
            pltpu.VMEM(turned, BF16),
            pltpu.VMEM((8, 8, ROWS), F32),
            pltpu.VMEM((8, 8, ROWS), F32),
            pltpu.VMEM((16, ROWS), F32),
            pltpu.VMEM((8, 16, ROWS), F32),
            pltpu.VMEM((4, HD, ROWS), BF16),
            pltpu.VMEM(turned, BF16),
            pltpu.VMEM(turned, BF16),
            pltpu.VMEM(block, BF16),
            pltpu.VMEM(block, BF16),
            pltpu.VMEM(block, BF16),
            pltpu.VMEM(block, BF16),
            pltpu.VMEM((8, HALF, HD), BF16),
            pltpu.VMEM((8, HALF, HD), BF16),
            pltpu.VMEM((8, PIECE, HD), BF16),
            pltpu.VMEM((8, PIECE, HD), BF16),
            pltpu.SemaphoreType.DMA((15, 8)),
            pltpu.SemaphoreType.DMA((15, 8)),
            pltpu.SemaphoreType.DMA((5,)),
        ],
        compiler_params=pltpu.CompilerParams(
            collective_id=0,
            has_side_effects=True,
            vmem_limit_bytes=56 * 1024 * 1024,
        ),
    )(q, k, v, og, w)


def solution(mesh):
    torus = Mesh(mesh.devices.reshape(2, 2, 2, 4, 8), TENSOR + CONTEXT)
    tiles = P(CONTEXT, TENSOR)
    return jax.shard_map(
        local,
        mesh=torus,
        in_specs=(tiles, tiles, tiles, tiles, P(None, TENSOR)),
        out_specs=(tiles, tiles, tiles, tiles),
        check_vma=False,
    )
```

```python
import jax
import jax.numpy as jnp
from jax import lax
from jax.experimental import pallas as pl
from jax.experimental.pallas import tpu as pltpu
from jax.sharding import Mesh
from jax.sharding import PartitionSpec as P

HD = 128
ROWS = 256
TENSOR = ("tensor_0", "tensor_1")
CONTEXT = ("context_0", "context_1", "context_2")
SCALING = HD ** (-0.5)
SCORE_SCALE = SCALING * 1.4426950408889634
FEATURES = 1536
PIECE = 96

BF16 = jnp.bfloat16
F32 = jnp.float32

(Q, K, V, G, O, L, ST, DQ, DK, DV, W, PA, X, XC, AT, AC, S2) = range(17)
EARLY = 6
SUBSET = 192


def dot(a, b, ca, cb):
    return lax.dot_general(a, b, (((ca,), (cb,)), ((), ())), preferred_element_type=F32)


def fold(x, op):
    return op(x.reshape(x.shape[0] // 8, 8, x.shape[1]), axis=0)


Z_OFFSET = (0, 1, -1, 2, -2, 3, -3, 4)


def kernel(
    q_in, k_in, v_in, og_in, w_in,
    dq_out, dk_out, dv_out, dw_out,
    qg, kg, vg, kt, vt, og, ogt, wg, part, part_in, gt, gs,
    s_tile, powers, grads, shift, sums,
    o_send, o_in, l_send, l_in, st_send, st_in,
    xg, att, dq_send, dq_in, dk_send, dk_in, dv_send, dv_in,
    p_send, p_in,
    send, recv, here,
):
    xh = lax.axis_index("tensor_0")
    co = lax.axis_index("tensor_1")
    xl = lax.axis_index("context_0")
    y = lax.axis_index("context_1")
    z = lax.axis_index("context_2")

    def z_to(i):
        return {"context_2": lax.rem(z + Z_OFFSET[i] + 8, 8)}

    def z_back(i):
        return {"context_2": lax.rem(z - Z_OFFSET[i] + 8, 8)}

    def u_to(e):
        return {
            "context_0": lax.rem(xl + e // 4, 2),
            "context_1": lax.rem(y + e % 4, 4),
        }

    def u_back(e):
        return {
            "context_0": lax.rem(xl + e // 4, 2),
            "context_1": lax.rem(y + 4 - e % 4, 4),
        }

    def t_to(s):
        return {
            "tensor_0": lax.rem(xh + s // 2, 2),
            "tensor_1": lax.rem(co + s % 2, 2),
        }

    def w_to(s):
        target = t_to(s)
        if s // 2:
            target["context_0"] = 1 - xl
        return target

    def remote(src, dst, row, slot, target, recv_slot=None):
        return pltpu.make_async_remote_copy(
            src_ref=src,
            dst_ref=dst,
            send_sem=send.at[row, slot],
            recv_sem=recv.at[row, slot if recv_slot is None else recv_slot],
            device_id=target,
            device_id_type=pl.DeviceIdType.MESH,
        )

    def span(e, count=ROWS):
        return slice(e * count, (e + 1) * count)

    tensor_place = 2 * xh + co
    own_rows = [
        pltpu.make_async_copy(og_in, og, here.at[3]),
        pltpu.make_async_copy(
            w_in.at[pl.ds(pl.multiple_of(tensor_place * FEATURES, FEATURES), FEATURES)],
            wg.at[0],
            here.at[4],
        ),
        pltpu.make_async_copy(q_in, qg.at[span(0)], here.at[0]),
        pltpu.make_async_copy(k_in, kg.at[span(0)], here.at[1]),
        pltpu.make_async_copy(v_in, vg.at[span(0)], here.at[2]),
    ]
    for copy in own_rows:
        copy.start()

    barrier = pltpu.get_barrier_semaphore()

    def greet(target):
        pl.semaphore_signal(
            barrier, inc=1, device_id=target, device_id_type=pl.DeviceIdType.MESH
        )

    for i in range(7, 0, -1):
        greet(z_to(i))
        greet(u_to(i))
    for s in range(1, 4):
        greet(w_to(s))
    for copy in own_rows:
        copy.wait()
    for c in range(FEATURES // ROWS):
        ogt[span(c), :] = og[:, span(c)].astype(F32).T.astype(BF16)
    g_sum = dot(og[...], wg[0], 1, 0)
    own_subset = pl.multiple_of((xl * 4 + y) * SUBSET, SUBSET)
    xg[0, :, span(0)] = ogt[pl.ds(own_subset, SUBSET), :]
    pl.semaphore_wait(barrier, 17)

    def q_copy(i):
        source = {5: 3, 7: 3, 6: 4}.get(i, 0)
        target = {5: 1, 7: 3, 6: 2}.get(i, i)
        return remote(qg.at[span(source)], qg.at[span(i)], Q, i, z_to(target))

    def k_copy(e):
        return remote(k_in, kg.at[span(e)], K, e, u_to(e))

    def v_copy(e):
        return remote(v_in, vg.at[span(e)], V, e, u_to(e))

    def w_copy(s):
        place = 2 * lax.rem(xh + s // 2, 2) + lax.rem(co + s % 2, 2)
        block = w_in.at[pl.ds(pl.multiple_of(place * FEATURES, FEATURES), FEATURES)]
        return remote(block, wg.at[s], W, s, w_to(s))

    def x_copy(other, e):
        target = u_to(e)
        place = target["context_0"] * 4 + target["context_1"]
        block = ogt.at[pl.ds(pl.multiple_of(place * SUBSET, SUBSET), SUBSET)]
        if other:
            target["tensor_0"] = 1 - xh
        return remote(block, xg.at[other, :, span(e)], (X, XC)[other], e, target)

    near = (1, 3, 4, 5, 7, 2, 6)
    for i in (3, 4, 1, 2):
        q_copy(i).start()
    for e in near:
        k_copy(e).start()
    for s in (2, 3, 1):
        w_copy(s).start()
    for e in near:
        v_copy(e).start()
    for e in near:
        x_copy(0, e).start()

    q_copy(3).wait_recv()
    q_copy(5).start()
    q_copy(7).start()
    q_copy(4).wait_recv()
    q_copy(6).start()
    for e in near:
        k_copy(e).wait_recv()

    def o_copy(i):
        return remote(o_send.at[i], o_in.at[i], O, i, z_back(i))

    def l_copy(i):
        return remote(l_send.at[i], l_in.at[i], L, i, z_back(i))

    def score(i, j, top):
        scores = dot(kg[span(j), :], qg[span(i), :], 1, 1) * SCORE_SCALE
        s_tile[i % 2, span(j), :] = scores
        highest = fold(scores, jnp.max)
        return highest if top is None else jnp.maximum(top, highest)

    def give(i, weighted, row_total):
        o_send[i] = (weighted / row_total).astype(BF16)
        l_send[i] = jnp.broadcast_to(shift[i] + jnp.log2(row_total), (8, ROWS))
        if i:
            o_copy(i).start()
            l_copy(i).start()

    top = None
    for j in range(8):
        top = score(0, j, top)
    for i in range(8):
        if 3 != i + 1 != 4 and i < 7:
            q_copy(i + 1).wait_recv()
        row_shift = jnp.ceil(jnp.max(top, axis=0, keepdims=True))
        shift[i] = row_shift
        if i == EARLY:
            for e in near:
                v_copy(e).wait_recv()
            for e in range(8):
                vt[:, span(e)] = vg[span(e), :].astype(F32).T.astype(BF16)
            for h in range(EARLY - 1, -1, -1):
                give(h, dot(vt[...], powers[:, span(h)], 1, 0), sums[h])
        top = None
        total = jnp.zeros((8, ROWS), F32)
        weighted = jnp.zeros((HD, ROWS), F32)
        for j in range(8):
            if i < 7:
                top = score(i + 1, j, top)
            p = jnp.exp2(s_tile[i % 2, span(j), :] - row_shift)
            total = total + fold(p, jnp.sum)
            p = p.astype(BF16)
            powers[span(j), span(i)] = p
            if i >= EARLY:
                weighted = weighted + dot(vt[:, span(j)], p, 1, 0)
        row_total = jnp.sum(total, axis=0, keepdims=True)
        if i < EARLY:
            sums[i] = row_total
        else:
            give(i, weighted, row_total)

    def part_copy(s):
        return remote(part.at[s], part_in.at[s], PA, s, t_to(s))

    for s in (1, 2, 3):
        w_copy(s).wait_recv()
        part[s] = dot(og[...], wg[s], 1, 0).astype(BF16)
        part_copy(s).start()
    for e in (0,) + near:
        x_copy(1, e).start()
    for e in range(8):
        kt[:, span(e)] = kg[span(e), :].astype(F32).T.astype(BF16)
    for s in (1, 2, 3):
        part_copy(s).wait_recv()
        g_sum = g_sum + part_in[s].astype(F32)
    g_own = g_sum.T.astype(BF16)
    gt[0] = g_own

    def g_copy(i):
        source = {5: 3, 7: 3, 6: 4}.get(i, 0)
        target = {5: 1, 7: 3, 6: 2}.get(i, i)
        return remote(gt.at[source], gt.at[i], G, i, z_to(target))

    for i in (3, 4, 1, 2):
        g_copy(i).start()

    for i in range(1, 8):
        l_copy(i).wait_recv()
    log_parts = [l_send[0][0:1, :]] + [l_in[i][0:1, :] for i in range(1, 8)]
    highest = log_parts[0]
    for value in log_parts[1:]:
        highest = jnp.maximum(highest, value)
    factors = [jnp.exp2(value - highest) for value in log_parts]
    total = factors[0]
    for value in factors[1:]:
        total = total + value
    joined = (factors[0] / total) * o_send[0].astype(F32)
    for i in range(1, 8):
        o_copy(i).wait_recv()
        joined = joined + (factors[i] / total) * o_in[i].astype(F32)
    attended = joined.astype(BF16)
    att[span(0, HD), span(0)] = attended

    log_total = highest + jnp.log2(total)
    row_delta = jnp.sum(attended.astype(F32) * g_own.astype(F32), axis=0, keepdims=True)
    st_send[0:8, :] = jnp.broadcast_to(log_total, (8, ROWS))
    st_send[8:16, :] = jnp.broadcast_to(row_delta, (8, ROWS))
    st_in[0] = st_send[...]

    def st_copy(i):
        return remote(st_send, st_in.at[i], ST, i, z_to(i))

    for i in range(1, 8):
        st_copy(i).start()

    def a_copy(other, e):
        target = u_to(e)
        if other:
            target["tensor_1"] = 1 - co
        return remote(
            att.at[span(0, HD), span(0)],
            att.at[span(other, HD), span(e)],
            (AT, AC)[other],
            e,
            target,
        )

    for e in (0,) + near:
        if e:
            a_copy(0, e).start()
        a_copy(1, e).start()
    g_copy(3).wait_recv()
    g_copy(5).start()
    g_copy(7).start()
    g_copy(4).wait_recv()
    g_copy(6).start()

    def dq_copy(i):
        return remote(dq_send.at[i], dq_in.at[i], DQ, i, z_back(i))

    for i in range(8):
        if i:
            if 3 != i != 4:
                g_copy(i).wait_recv()
            st_copy(i).wait_recv()
        factor = jnp.exp2(shift[i] - st_in[i, 0:1, :])
        delta = factor * st_in[i, 8:9, :]
        g_block = (gt[i].astype(F32) * factor).astype(BF16)
        gs[:, span(i)] = g_block
        query_sum = jnp.zeros((HD, ROWS), F32)
        for j in range(8):
            prob = dot(vg[span(j), :], g_block, 1, 0)
            slope = ((prob - delta) * powers[span(j), span(i)].astype(F32)).astype(BF16)
            grads[span(j), span(i)] = slope
            query_sum = query_sum + dot(kt[:, span(j)], slope, 1, 0)
        dq_send[i] = query_sum.astype(BF16)
        if i:
            dq_copy(i).start()

    def dk_copy(e):
        return remote(dk_send.at[e], dk_in.at[e], DK, e, u_back(e))

    def dv_copy(e):
        return remote(dv_send.at[e], dv_in.at[e], DV, e, u_back(e))

    def key_side(e):
        dk_send[e] = dot(grads[span(e), :], qg[...], 1, 0).astype(BF16)
        if e:
            dk_copy(e).start()
        dv_send[e] = dot(powers[span(e), :], gs[...], 1, 1).astype(BF16)
        if e:
            dv_copy(e).start()

    for e in (6, 2, 7, 5):
        key_side(e)

    self_served = jnp.logical_and(
        jnp.logical_and(co == lax.div(y, 2), xl == lax.rem(y, 2)), y == lax.div(z, 2)
    )

    def p_copy(n):
        target = {
            "tensor_1": lax.rem(co + n % 2, 2),
            "context_0": lax.rem(xh + n // 4, 2),
            "context_1": 2 * co + xl,
            "context_2": 2 * y + n // 2 % 2,
        }
        return remote(p_send.at[n], p_in.at[z], S2, n, target, z)

    def p_own(n):
        if n % 2:
            return False
        same = jnp.logical_and(lax.rem(xh + n // 4, 2) == xl, lax.rem(z, 2) == n // 2 % 2)
        return jnp.logical_and(self_served, same)

    for e in (0,) + near:
        if e:
            x_copy(0, e).wait_recv()
            a_copy(0, e).wait_recv()
        x_copy(1, e).wait_recv()
        a_copy(1, e).wait_recv()
    for t in range(2):
        product = dot(xg[t], att[...], 1, 1).astype(BF16)
        for r in range(2):
            for c in range(2):
                n = 4 * t + 2 * r + c
                p_send[n] = product[span(r, PIECE), span(c, HD)]
                if c:
                    p_copy(n).start()
                else:
                    @pl.when(jnp.logical_not(p_own(n)))
                    def _(n=n):
                        p_copy(n).start()

                    @pl.when(p_own(n))
                    def _(n=n):
                        p_in[z] = p_send[n]

    for e in (4, 3, 1, 0):
        key_side(e)

    total = dq_send[0].astype(F32)
    for i in range(1, 8):
        dq_copy(i).wait_recv()
        total = total + dq_in[i].astype(F32)
    dq_out[...] = (total * SCALING).T.astype(BF16)
    for n in range(8):
        @pl.when(jnp.logical_not(jnp.logical_and(self_served, z == n)))
        def _(n=n):
            remote(p_send.at[n], p_in.at[n], S2, n, z_to(1)).wait_recv()

    total = p_in[0].astype(F32)
    for n in range(1, 8):
        total = total + p_in[n].astype(F32)
    dw_out[...] = total
    total = dk_send[0].astype(F32)
    for e in range(1, 8):
        dk_copy(e).wait_recv()
        total = total + dk_in[e].astype(F32)
    dk_out[...] = (total * SCALING).astype(BF16)
    total = dv_send[0].astype(F32)
    for e in range(1, 8):
        dv_copy(e).wait_recv()
        total = total + dv_in[e].astype(F32)
    dv_out[...] = total.astype(BF16)

    for i in range(1, 8):
        for copy in (q_copy, k_copy, v_copy, g_copy, o_copy, l_copy, st_copy, dq_copy, dk_copy,
                     dv_copy):
            copy(i).wait_send()
        x_copy(0, i).wait_send()
        a_copy(0, i).wait_send()
    for i in range(8):
        x_copy(1, i).wait_send()
        a_copy(1, i).wait_send()
    for s in range(1, 4):
        w_copy(s).wait_send()
        part_copy(s).wait_send()
    for n in range(8):
        if n % 2:
            p_copy(n).wait_send()
        else:
            @pl.when(jnp.logical_not(p_own(n)))
            def _(n=n):
                p_copy(n).wait_send()


def hand_over(*refs):
    for source, target in zip(refs[:4], refs[4:]):
        target[...] = source[...]


def local(q, k, v, og, w):
    anywhere = pl.BlockSpec(memory_space=pl.ANY)
    vmem = pl.BlockSpec(memory_space=pltpu.VMEM)
    tokens = 8 * ROWS
    block = (8, ROWS, HD)
    turned = (8, HD, ROWS)
    shapes = (
        jax.ShapeDtypeStruct((ROWS, HD), BF16),
        jax.ShapeDtypeStruct((ROWS, HD), BF16),
        jax.ShapeDtypeStruct((ROWS, HD), BF16),
        jax.ShapeDtypeStruct((PIECE, HD), F32),
    )
    results = pl.pallas_call(
        kernel,
        out_shape=shapes,
        in_specs=[anywhere] * 5,
        out_specs=(vmem,) * 4,
        scratch_shapes=[
            pltpu.VMEM((tokens, HD), BF16),
            pltpu.VMEM((tokens, HD), BF16),
            pltpu.VMEM((tokens, HD), BF16),
            pltpu.VMEM((HD, tokens), BF16),
            pltpu.VMEM((HD, tokens), BF16),
            pltpu.VMEM((ROWS, FEATURES), BF16),
            pltpu.VMEM((FEATURES, ROWS), BF16),
            pltpu.VMEM((4, FEATURES, HD), BF16),
            pltpu.VMEM((4, ROWS, HD), BF16),
            pltpu.VMEM((4, ROWS, HD), BF16),
            pltpu.VMEM(turned, BF16),
            pltpu.VMEM((HD, tokens), BF16),
            pltpu.VMEM((2, tokens, ROWS), F32),
            pltpu.VMEM((tokens, tokens), BF16),
            pltpu.VMEM((tokens, tokens), BF16),
            pltpu.VMEM((8, 1, ROWS), F32),
            pltpu.VMEM((8, 1, ROWS), F32),
            pltpu.VMEM(turned, BF16),
            pltpu.VMEM(turned, BF16),
            pltpu.VMEM((8, 8, ROWS), F32),
            pltpu.VMEM((8, 8, ROWS), F32),
            pltpu.VMEM((16, ROWS), F32),
            pltpu.VMEM((8, 16, ROWS), F32),
            pltpu.VMEM((2, SUBSET, tokens), BF16),
            pltpu.VMEM((2 * HD, tokens), BF16),
            pltpu.VMEM(turned, BF16),
            pltpu.VMEM(turned, BF16),
            pltpu.VMEM(block, BF16),
            pltpu.VMEM(block, BF16),
            pltpu.VMEM(block, BF16),
            pltpu.VMEM(block, BF16),
            pltpu.VMEM((8, PIECE, HD), BF16),
            pltpu.VMEM((8, PIECE, HD), BF16),
            pltpu.SemaphoreType.DMA((17, 8)),
            pltpu.SemaphoreType.DMA((17, 8)),
            pltpu.SemaphoreType.DMA((5,)),
        ],
        compiler_params=pltpu.CompilerParams(
            collective_id=0,
            has_side_effects=True,
            vmem_limit_bytes=56 * 1024 * 1024,
        ),
    )(q, k, v, og, w)
    return pl.pallas_call(
        hand_over,
        out_shape=shapes,
        in_specs=[vmem] * 4,
        out_specs=(vmem,) * 4,
    )(*results)


def solution(mesh):
    torus = Mesh(mesh.devices.reshape(2, 2, 2, 4, 8), TENSOR + CONTEXT)
    tiles = P(CONTEXT, TENSOR)
    return jax.shard_map(
        local,
        mesh=torus,
        in_specs=(tiles, tiles, tiles, tiles, P(None, TENSOR)),
        out_specs=(tiles, tiles, tiles, tiles),
        check_vma=False,
    )
```

```python
import jax
import jax.numpy as jnp
from jax import lax
from jax.experimental import pallas as pl
from jax.experimental.pallas import tpu as pltpu
from jax.sharding import Mesh
from jax.sharding import PartitionSpec as P

HD = 128
ROWS = 256
TENSOR = ("tensor_0", "tensor_1")
CONTEXT = ("context_0", "context_1", "context_2")
SCALING = HD ** (-0.5)
SCORE_SCALE = SCALING * 1.4426950408889634
FEATURES = 1536
PIECE = 96

BF16 = jnp.bfloat16
F32 = jnp.float32

(Q, K, V, G, O, L, ST, DQ, DK, DV, W, PA, X, XC, AT, AC, S2) = range(17)
EARLY = 6
SUBSET = 192


def dot(a, b, ca, cb):
    return lax.dot_general(a, b, (((ca,), (cb,)), ((), ())), preferred_element_type=F32)


def fold(x, op):
    return op(x.reshape(x.shape[0] // 8, 8, x.shape[1]), axis=0)


Z_OFFSET = (0, 1, -1, 2, -2, 3, -3, 4)


def kernel(
    q_in, k_in, v_in, og_in, w_in,
    dq_out, dk_out, dv_out, dw_out,
    qg, kg, vg, kt, vt, og, ogt, wg, part, part_in, gt, gs,
    s_tile, powers, grads, shift, sums,
    o_send, o_in, l_send, l_in, st_send, st_in,
    xg, att, dq_send, dq_in, dk_send, dk_in, dv_send, dv_in,
    p_send, p_in,
    send, recv, here,
):
    xh = lax.axis_index("tensor_0")
    co = lax.axis_index("tensor_1")
    xl = lax.axis_index("context_0")
    y = lax.axis_index("context_1")
    z = lax.axis_index("context_2")

    def z_to(i):
        return {"context_2": lax.rem(z + Z_OFFSET[i] + 8, 8)}

    def z_back(i):
        return {"context_2": lax.rem(z - Z_OFFSET[i] + 8, 8)}

    def u_to(e):
        return {
            "context_0": lax.rem(xl + e // 4, 2),
            "context_1": lax.rem(y + e % 4, 4),
        }

    def u_back(e):
        return {
            "context_0": lax.rem(xl + e // 4, 2),
            "context_1": lax.rem(y + 4 - e % 4, 4),
        }

    def t_to(s):
        return {
            "tensor_0": lax.rem(xh + s // 2, 2),
            "tensor_1": lax.rem(co + s % 2, 2),
        }

    def w_to(s):
        target = t_to(s)
        if s // 2:
            target["context_0"] = 1 - xl
        return target

    def remote(src, dst, row, slot, target, recv_slot=None):
        return pltpu.make_async_remote_copy(
            src_ref=src,
            dst_ref=dst,
            send_sem=send.at[row, slot],
            recv_sem=recv.at[row, slot if recv_slot is None else recv_slot],
            device_id=target,
            device_id_type=pl.DeviceIdType.MESH,
        )

    def span(e, count=ROWS):
        return slice(e * count, (e + 1) * count)

    def pair(row, half):
        return lax.rem(row + lax.div(z, 2) + 2 * half, 4)

    tensor_place = 2 * xh + co
    own_rows = [
        pltpu.make_async_copy(og_in, og, here.at[3]),
        pltpu.make_async_copy(
            w_in.at[pl.ds(pl.multiple_of(tensor_place * FEATURES, FEATURES), FEATURES)],
            wg.at[0],
            here.at[4],
        ),
        pltpu.make_async_copy(q_in, qg.at[span(0)], here.at[0]),
        pltpu.make_async_copy(k_in, kg.at[span(0)], here.at[1]),
        pltpu.make_async_copy(v_in, vg.at[span(0)], here.at[2]),
    ]
    for copy in own_rows:
        copy.start()

    barrier = pltpu.get_barrier_semaphore()

    def greet(target):
        pl.semaphore_signal(
            barrier, inc=1, device_id=target, device_id_type=pl.DeviceIdType.MESH
        )

    for i in range(7, 0, -1):
        greet(z_to(i))
        greet(u_to(i))
    for s in range(1, 4):
        greet(w_to(s))
    for copy in own_rows:
        copy.wait()
    for c in range(FEATURES // ROWS):
        ogt[span(c), :] = og[:, span(c)].astype(F32).T.astype(BF16)
    g_sum = dot(og[...], wg[0], 1, 0)
    own_subset = pl.multiple_of((xl * 4 + pair(y, xh)) * SUBSET, SUBSET)
    xg[0, :, span(0)] = ogt[pl.ds(own_subset, SUBSET), :]
    pl.semaphore_wait(barrier, 17)

    def q_copy(i):
        source = {5: 3, 7: 3, 6: 4}.get(i, 0)
        target = {5: 1, 7: 3, 6: 2}.get(i, i)
        return remote(qg.at[span(source)], qg.at[span(i)], Q, i, z_to(target))

    def k_copy(e):
        return remote(k_in, kg.at[span(e)], K, e, u_to(e))

    def v_copy(e):
        return remote(v_in, vg.at[span(e)], V, e, u_to(e))

    def w_copy(s):
        place = 2 * lax.rem(xh + s // 2, 2) + lax.rem(co + s % 2, 2)
        block = w_in.at[pl.ds(pl.multiple_of(place * FEATURES, FEATURES), FEATURES)]
        return remote(block, wg.at[s], W, s, w_to(s))

    def x_copy(e):
        target = u_to(e)
        place = target["context_0"] * 4 + pair(target["context_1"], xh)
        block = ogt.at[pl.ds(pl.multiple_of(place * SUBSET, SUBSET), SUBSET)]
        return remote(block, xg.at[0, :, span(e)], X, e, target)

    def x_pass(half):
        return remote(
            xg.at[0, :, span(half, 4 * ROWS)],
            xg.at[1, :, span(1 - half, 4 * ROWS)],
            XC,
            half,
            w_to(2),
            1 - half,
        )

    near = (1, 3, 4, 5, 7, 2, 6)
    for i in (3, 4, 1, 2):
        q_copy(i).start()
    for e in near:
        k_copy(e).start()
    for s in (2, 3, 1):
        w_copy(s).start()
    for e in near:
        v_copy(e).start()
    for e in near:
        x_copy(e).start()

    q_copy(3).wait_recv()
    q_copy(5).start()
    q_copy(7).start()
    q_copy(4).wait_recv()
    q_copy(6).start()
    for e in near:
        k_copy(e).wait_recv()

    def o_copy(i):
        return remote(o_send.at[i], o_in.at[i], O, i, z_back(i))

    def l_copy(i):
        return remote(l_send.at[i], l_in.at[i], L, i, z_back(i))

    def score(i, j, top):
        scores = dot(kg[span(j), :], qg[span(i), :], 1, 1) * SCORE_SCALE
        s_tile[i % 2, span(j), :] = scores
        highest = fold(scores, jnp.max)
        return highest if top is None else jnp.maximum(top, highest)

    def give(i, weighted, row_total):
        o_send[i] = (weighted / row_total).astype(BF16)
        l_send[i] = jnp.broadcast_to(shift[i] + jnp.log2(row_total), (8, ROWS))
        if i:
            o_copy(i).start()
            l_copy(i).start()

    top = None
    for j in range(8):
        top = score(0, j, top)
    for i in range(8):
        if 3 != i + 1 != 4 and i < 7:
            q_copy(i + 1).wait_recv()
        row_shift = jnp.ceil(jnp.max(top, axis=0, keepdims=True))
        shift[i] = row_shift
        if i == EARLY:
            for e in near:
                v_copy(e).wait_recv()
            for e in range(8):
                vt[:, span(e)] = vg[span(e), :].astype(F32).T.astype(BF16)
            for h in range(EARLY - 1, -1, -1):
                give(h, dot(vt[...], powers[:, span(h)], 1, 0), sums[h])
        top = None
        total = jnp.zeros((8, ROWS), F32)
        weighted = jnp.zeros((HD, ROWS), F32)
        for j in range(8):
            if i < 7:
                top = score(i + 1, j, top)
            p = jnp.exp2(s_tile[i % 2, span(j), :] - row_shift)
            total = total + fold(p, jnp.sum)
            p = p.astype(BF16)
            powers[span(j), span(i)] = p
            if i >= EARLY:
                weighted = weighted + dot(vt[:, span(j)], p, 1, 0)
        row_total = jnp.sum(total, axis=0, keepdims=True)
        if i < EARLY:
            sums[i] = row_total
        else:
            give(i, weighted, row_total)

    def part_copy(s):
        return remote(part.at[s], part_in.at[s], PA, s, t_to(s))

    for s in (1, 2, 3):
        w_copy(s).wait_recv()
        part[s] = dot(og[...], wg[s], 1, 0).astype(BF16)
        part_copy(s).start()
    for e in near:
        x_copy(e).wait_recv()
    for half in range(2):
        x_pass(half).start()
    for e in range(8):
        kt[:, span(e)] = kg[span(e), :].astype(F32).T.astype(BF16)
    for s in (1, 2, 3):
        part_copy(s).wait_recv()
        g_sum = g_sum + part_in[s].astype(F32)
    g_own = g_sum.T.astype(BF16)
    gt[0] = g_own

    def g_copy(i):
        source = {5: 3, 7: 3, 6: 4}.get(i, 0)
        target = {5: 1, 7: 3, 6: 2}.get(i, i)
        return remote(gt.at[source], gt.at[i], G, i, z_to(target))

    for i in (3, 4, 1, 2):
        g_copy(i).start()

    for i in range(1, 8):
        l_copy(i).wait_recv()
    log_parts = [l_send[0][0:1, :]] + [l_in[i][0:1, :] for i in range(1, 8)]
    highest = log_parts[0]
    for value in log_parts[1:]:
        highest = jnp.maximum(highest, value)
    factors = [jnp.exp2(value - highest) for value in log_parts]
    total = factors[0]
    for value in factors[1:]:
        total = total + value
    joined = (factors[0] / total) * o_send[0].astype(F32)
    for i in range(1, 8):
        o_copy(i).wait_recv()
        joined = joined + (factors[i] / total) * o_in[i].astype(F32)
    attended = joined.astype(BF16)
    att[span(0, HD), span(0)] = attended

    log_total = highest + jnp.log2(total)
    row_delta = jnp.sum(attended.astype(F32) * g_own.astype(F32), axis=0, keepdims=True)
    st_send[0:8, :] = jnp.broadcast_to(log_total, (8, ROWS))
    st_send[8:16, :] = jnp.broadcast_to(row_delta, (8, ROWS))
    st_in[0] = st_send[...]

    def st_copy(i):
        return remote(st_send, st_in.at[i], ST, i, z_to(i))

    for i in range(1, 8):
        st_copy(i).start()

    def a_copy(e):
        own = att.at[span(0, HD), span(0)]
        return remote(own, att.at[span(0, HD), span(e)], AT, e, u_to(e))

    def a_pass():
        return remote(att.at[span(0, HD)], att.at[span(1, HD)], AC, 0, t_to(1))

    for e in near:
        a_copy(e).start()
    g_copy(3).wait_recv()
    g_copy(5).start()
    g_copy(7).start()
    g_copy(4).wait_recv()
    g_copy(6).start()

    def dq_copy(i):
        return remote(dq_send.at[i], dq_in.at[i], DQ, i, z_back(i))

    def weigh(i):
        if i:
            if 3 != i != 4:
                g_copy(i).wait_recv()
            st_copy(i).wait_recv()
        factor = jnp.exp2(shift[i] - st_in[i, 0:1, :])
        sums[i] = factor * st_in[i, 8:9, :]
        gs[:, span(i)] = (gt[i].astype(F32) * factor).astype(BF16)

    def query_side(i):
        delta = sums[i]
        g_block = gs[:, span(i)]
        query_sum = jnp.zeros((HD, ROWS), F32)
        for j in range(8):
            prob = dot(vg[span(j), :], g_block, 1, 0)
            slope = ((prob - delta) * powers[span(j), span(i)].astype(F32)).astype(BF16)
            grads[span(j), span(i)] = slope
            query_sum = query_sum + dot(kt[:, span(j)], slope, 1, 0)
        dq_send[i] = query_sum.astype(BF16)
        if i:
            dq_copy(i).start()

    def dk_copy(e):
        return remote(dk_send.at[e], dk_in.at[e], DK, e, u_back(e))

    def dv_copy(e):
        return remote(dv_send.at[e], dv_in.at[e], DV, e, u_back(e))

    for i in (1, 2, 0, 3):
        weigh(i)
        query_side(i)
    for i in range(4, 8):
        weigh(i)
    for e in (6, 2, 7, 5, 4, 3, 1, 0):
        dv_send[e] = dot(powers[span(e), :], gs[...], 1, 1).astype(BF16)
        if e:
            dv_copy(e).start()
    for e in near:
        a_copy(e).wait_recv()
    a_pass().start()
    for i in (7, 5, 6, 4):
        query_side(i)

    self_served = jnp.logical_and(
        jnp.logical_and(co == lax.div(y, 2), xh == lax.rem(y, 2)), y == 2 * xl
    )

    def p_copy(n):
        target = {
            "tensor_1": lax.rem(co + n % 2, 2),
            "context_0": lax.rem(xh + n // 4, 2),
            "context_1": 2 * co + lax.rem(xl + n // 4, 2),
            "context_2": 2 * pair(y, lax.rem(xh + n // 4, 2)) + n // 2 % 2,
        }
        return remote(p_send.at[n], p_in.at[z], S2, n, target, z)

    def p_own(n):
        if n % 2:
            return False
        same = jnp.logical_and(lax.rem(xh + n // 4, 2) == xl, lax.rem(z, 2) == n // 2 % 2)
        return jnp.logical_and(self_served, same)

    for half in range(2):
        x_pass(half).wait_recv()
    a_pass().wait_recv()
    for t in range(2):
        product = dot(xg[t], att[...], 1, 1).astype(BF16)
        for r in range(2):
            for c in range(2):
                n = 4 * t + 2 * r + c
                p_send[n] = product[span(r, PIECE), span(c, HD)]
                if c:
                    p_copy(n).start()
                else:
                    @pl.when(jnp.logical_not(p_own(n)))
                    def _(n=n):
                        p_copy(n).start()

                    @pl.when(p_own(n))
                    def _(n=n):
                        p_in[z] = p_send[n]

    for e in (6, 2, 7, 5, 4, 3, 1, 0):
        dk_send[e] = dot(grads[span(e), :], qg[...], 1, 0).astype(BF16)
        if e:
            dk_copy(e).start()

    total = dv_send[0].astype(F32)
    for e in range(1, 8):
        dv_copy(e).wait_recv()
        total = total + dv_in[e].astype(F32)
    dv_out[...] = total.astype(BF16)
    total = dq_send[0].astype(F32)
    for i in range(1, 8):
        dq_copy(i).wait_recv()
        total = total + dq_in[i].astype(F32)
    dq_out[...] = (total * SCALING).T.astype(BF16)
    for n in range(8):
        @pl.when(jnp.logical_not(jnp.logical_and(self_served, z == n)))
        def _(n=n):
            remote(p_send.at[n], p_in.at[n], S2, n, z_to(1)).wait_recv()

    total = p_in[0].astype(F32)
    for n in range(1, 8):
        total = total + p_in[n].astype(F32)
    dw_out[...] = total
    total = dk_send[0].astype(F32)
    for e in range(1, 8):
        dk_copy(e).wait_recv()
        total = total + dk_in[e].astype(F32)
    dk_out[...] = (total * SCALING).astype(BF16)

    for i in range(1, 8):
        for copy in (q_copy, k_copy, v_copy, g_copy, o_copy, l_copy, st_copy, dq_copy, dk_copy,
                     dv_copy):
            copy(i).wait_send()
        x_copy(i).wait_send()
        a_copy(i).wait_send()
    a_pass().wait_send()
    for half in range(2):
        x_pass(half).wait_send()
    for s in range(1, 4):
        w_copy(s).wait_send()
        part_copy(s).wait_send()
    for n in range(8):
        if n % 2:
            p_copy(n).wait_send()
        else:
            @pl.when(jnp.logical_not(p_own(n)))
            def _(n=n):
                p_copy(n).wait_send()


def hand_over(*refs):
    for source, target in zip(refs[:4], refs[4:]):
        target[...] = source[...]


def local(q, k, v, og, w):
    anywhere = pl.BlockSpec(memory_space=pl.ANY)
    vmem = pl.BlockSpec(memory_space=pltpu.VMEM)
    tokens = 8 * ROWS
    block = (8, ROWS, HD)
    turned = (8, HD, ROWS)
    shapes = (
        jax.ShapeDtypeStruct((ROWS, HD), BF16),
        jax.ShapeDtypeStruct((ROWS, HD), BF16),
        jax.ShapeDtypeStruct((ROWS, HD), BF16),
        jax.ShapeDtypeStruct((PIECE, HD), F32),
    )
    results = pl.pallas_call(
        kernel,
        out_shape=shapes,
        in_specs=[anywhere] * 5,
        out_specs=(vmem,) * 4,
        scratch_shapes=[
            pltpu.VMEM((tokens, HD), BF16),
            pltpu.VMEM((tokens, HD), BF16),
            pltpu.VMEM((tokens, HD), BF16),
            pltpu.VMEM((HD, tokens), BF16),
            pltpu.VMEM((HD, tokens), BF16),
            pltpu.VMEM((ROWS, FEATURES), BF16),
            pltpu.VMEM((FEATURES, ROWS), BF16),
            pltpu.VMEM((4, FEATURES, HD), BF16),
            pltpu.VMEM((4, ROWS, HD), BF16),
            pltpu.VMEM((4, ROWS, HD), BF16),
            pltpu.VMEM(turned, BF16),
            pltpu.VMEM((HD, tokens), BF16),
            pltpu.VMEM((2, tokens, ROWS), F32),
            pltpu.VMEM((tokens, tokens), BF16),
            pltpu.VMEM((tokens, tokens), BF16),
            pltpu.VMEM((8, 1, ROWS), F32),
            pltpu.VMEM((8, 1, ROWS), F32),
            pltpu.VMEM(turned, BF16),
            pltpu.VMEM(turned, BF16),
            pltpu.VMEM((8, 8, ROWS), F32),
            pltpu.VMEM((8, 8, ROWS), F32),
            pltpu.VMEM((16, ROWS), F32),
            pltpu.VMEM((8, 16, ROWS), F32),
            pltpu.VMEM((2, SUBSET, tokens), BF16),
            pltpu.VMEM((2 * HD, tokens), BF16),
            pltpu.VMEM(turned, BF16),
            pltpu.VMEM(turned, BF16),
            pltpu.VMEM(block, BF16),
            pltpu.VMEM(block, BF16),
            pltpu.VMEM(block, BF16),
            pltpu.VMEM(block, BF16),
            pltpu.VMEM((8, PIECE, HD), BF16),
            pltpu.VMEM((8, PIECE, HD), BF16),
            pltpu.SemaphoreType.DMA((17, 8)),
            pltpu.SemaphoreType.DMA((17, 8)),
            pltpu.SemaphoreType.DMA((5,)),
        ],
        compiler_params=pltpu.CompilerParams(
            collective_id=0,
            has_side_effects=True,
            vmem_limit_bytes=56 * 1024 * 1024,
        ),
    )(q, k, v, og, w)
    return pl.pallas_call(
        hand_over,
        out_shape=shapes,
        in_specs=[vmem] * 4,
        out_specs=(vmem,) * 4,
    )(*results)


def solution(mesh):
    torus = Mesh(mesh.devices.reshape(2, 2, 2, 4, 8), TENSOR + CONTEXT)
    tiles = P(CONTEXT, TENSOR)
    return jax.shard_map(
        local,
        mesh=torus,
        in_specs=(tiles, tiles, tiles, tiles, P(None, TENSOR)),
        out_specs=(tiles, tiles, tiles, tiles),
        check_vma=False,
    )
```

```python
import jax
import jax.numpy as jnp
from jax import lax
from jax.experimental import pallas as pl
from jax.experimental.pallas import tpu as pltpu
from jax.sharding import Mesh
from jax.sharding import PartitionSpec as P

HD = 128
ROWS = 256
TENSOR = ("tensor_0", "tensor_1")
CONTEXT = ("context_0", "context_1", "context_2")
SCALING = HD ** (-0.5)
SCORE_SCALE = SCALING * 1.4426950408889634
FEATURES = 1536
PIECE = 96

BF16 = jnp.bfloat16
F32 = jnp.float32

(Q, K, V, G, O, L, ST, DQ, DK, DV, W, PA, X, XC, AT, AC, S2) = range(17)
EARLY = 3
SUBSET = 192


def dot(a, b, ca, cb):
    return lax.dot_general(a, b, (((ca,), (cb,)), ((), ())), preferred_element_type=F32)


def fold(x, op):
    return op(x.reshape(x.shape[0] // 8, 8, x.shape[1]), axis=0)


Z_OFFSET = (0, 1, -1, 2, -2, 3, -3, 4)


def kernel(
    q_in, k_in, v_in, og_in, w_in,
    dq_out, dk_out, dv_out, dw_out,
    qg, kg, vg, kt, vt, og, ogt, wg, part, part_in, gt, gs,
    s_tile, powers, grads, shift, sums,
    o_send, o_in, l_send, l_in, st_send, st_in,
    xg, att, dq_send, dq_in, dk_send, dk_in, dv_send, dv_in,
    p_send, p_in,
    send, recv, here,
):
    xh = lax.axis_index("tensor_0")
    co = lax.axis_index("tensor_1")
    xl = lax.axis_index("context_0")
    y = lax.axis_index("context_1")
    z = lax.axis_index("context_2")

    def z_to(i):
        return {"context_2": lax.rem(z + Z_OFFSET[i] + 8, 8)}

    def z_back(i):
        return {"context_2": lax.rem(z - Z_OFFSET[i] + 8, 8)}

    def u_to(e):
        return {
            "context_0": lax.rem(xl + e // 4, 2),
            "context_1": lax.rem(y + e % 4, 4),
        }

    def u_back(e):
        return {
            "context_0": lax.rem(xl + e // 4, 2),
            "context_1": lax.rem(y + 4 - e % 4, 4),
        }

    def t_to(s):
        return {
            "tensor_0": lax.rem(xh + s // 2, 2),
            "tensor_1": lax.rem(co + s % 2, 2),
        }

    def w_to(s):
        target = t_to(s)
        if s // 2:
            target["context_0"] = 1 - xl
        return target

    def remote(src, dst, row, slot, target, recv_slot=None):
        return pltpu.make_async_remote_copy(
            src_ref=src,
            dst_ref=dst,
            send_sem=send.at[row, slot],
            recv_sem=recv.at[row, slot if recv_slot is None else recv_slot],
            device_id=target,
            device_id_type=pl.DeviceIdType.MESH,
        )

    def span(e, count=ROWS):
        return slice(e * count, (e + 1) * count)

    def pair(row, half):
        return lax.rem(row + lax.div(z, 2) + 2 * half, 4)

    tensor_place = 2 * xh + co
    own_rows = [
        pltpu.make_async_copy(og_in, og, here.at[3]),
        pltpu.make_async_copy(
            w_in.at[pl.ds(pl.multiple_of(tensor_place * FEATURES, FEATURES), FEATURES)],
            wg.at[0],
            here.at[4],
        ),
        pltpu.make_async_copy(q_in, qg.at[span(0)], here.at[0]),
        pltpu.make_async_copy(k_in, kg.at[span(0)], here.at[1]),
        pltpu.make_async_copy(v_in, vg.at[span(0)], here.at[2]),
    ]
    for copy in own_rows:
        copy.start()

    barrier = pltpu.get_barrier_semaphore()

    def greet(target):
        pl.semaphore_signal(
            barrier, inc=1, device_id=target, device_id_type=pl.DeviceIdType.MESH
        )

    for i in range(7, 0, -1):
        greet(z_to(i))
        greet(u_to(i))
    for s in range(1, 4):
        greet(w_to(s))
    for copy in own_rows:
        copy.wait()
    for c in range(FEATURES // ROWS):
        ogt[span(c), :] = og[:, span(c)].astype(F32).T.astype(BF16)
    g_sum = dot(og[...], wg[0], 1, 0)
    own_subset = pl.multiple_of((xl * 4 + pair(y, xh)) * SUBSET, SUBSET)
    xg[0, :, span(0)] = ogt[pl.ds(own_subset, SUBSET), :]
    pl.semaphore_wait(barrier, 17)

    def q_copy(i):
        source = {5: 3, 7: 3, 6: 4}.get(i, 0)
        target = {5: 1, 7: 3, 6: 2}.get(i, i)
        return remote(qg.at[span(source)], qg.at[span(i)], Q, i, z_to(target))

    def k_copy(e):
        if e > 4:
            return remote(kg.at[span(e - 4)], kg.at[span(e)], K, e, u_to(4))
        return remote(kg.at[span(0)], kg.at[span(e)], K, e, u_to(e))

    def v_copy(e):
        if e > 4:
            return remote(vg.at[span(4)], vg.at[span(e)], V, e, u_to(e - 4))
        return remote(vg.at[span(0)], vg.at[span(e)], V, e, u_to(e))

    def w_copy(s):
        place = 2 * lax.rem(xh + s // 2, 2) + lax.rem(co + s % 2, 2)
        block = w_in.at[pl.ds(pl.multiple_of(place * FEATURES, FEATURES), FEATURES)]
        return remote(block, wg.at[s], W, s, w_to(s))

    def x_copy(e):
        target = u_to(e)
        place = target["context_0"] * 4 + pair(target["context_1"], xh)
        block = ogt.at[pl.ds(pl.multiple_of(place * SUBSET, SUBSET), SUBSET)]
        return remote(block, xg.at[0, :, span(e)], X, e, target)

    def x_pass(half):
        return remote(
            xg.at[0, :, span(half, 4 * ROWS)],
            xg.at[1, :, span(1 - half, 4 * ROWS)],
            XC,
            half,
            w_to(2),
            1 - half,
        )

    near = (1, 3, 4, 5, 7, 2, 6)
    for e in (1, 3, 4):
        k_copy(e).start()
    for i in (3, 4, 1, 2):
        q_copy(i).start()
    v_copy(4).start()
    k_copy(2).start()
    for s in (2, 3, 1):
        w_copy(s).start()
    for e in (1, 3, 2):
        v_copy(e).start()

    for e in (1, 3):
        k_copy(e).wait_recv()
        k_copy(e + 4).start()
    q_copy(3).wait_recv()
    q_copy(5).start()
    q_copy(7).start()
    q_copy(4).wait_recv()
    q_copy(6).start()
    k_copy(2).wait_recv()
    k_copy(6).start()
    v_copy(4).wait_recv()
    for e in (5, 7, 6):
        v_copy(e).start()
    for e in near:
        x_copy(e).start()
    for e in (4, 5, 7, 6):
        k_copy(e).wait_recv()

    def o_copy(i):
        return remote(o_send.at[i], o_in.at[i], O, i, z_back(i))

    def l_copy(i):
        return remote(l_send.at[i], l_in.at[i], L, i, z_back(i))

    def score(i, j, top):
        scores = dot(kg[span(j), :], qg[span(i), :], 1, 1) * SCORE_SCALE
        s_tile[i % 2, span(j), :] = scores
        highest = fold(scores, jnp.max)
        return highest if top is None else jnp.maximum(top, highest)

    def give(i, weighted, row_total):
        o_send[i] = (weighted / row_total).astype(BF16)
        l_send[i] = jnp.broadcast_to(shift[i] + jnp.log2(row_total), (8, ROWS))
        if i:
            o_copy(i).start()
            l_copy(i).start()

    top = None
    for j in range(8):
        top = score(0, j, top)
    for i in range(8):
        if 3 != i + 1 != 4 and i < 7:
            q_copy(i + 1).wait_recv()
        row_shift = jnp.ceil(jnp.max(top, axis=0, keepdims=True))
        shift[i] = row_shift
        if i == EARLY:
            for e in (1, 3, 2, 5, 7, 6):
                v_copy(e).wait_recv()
            for e in range(8):
                vt[:, span(e)] = vg[span(e), :].astype(F32).T.astype(BF16)
            for h in range(EARLY - 1, -1, -1):
                give(h, dot(vt[...], powers[:, span(h)], 1, 0), sums[h])
        top = None
        total = jnp.zeros((8, ROWS), F32)
        weighted = jnp.zeros((HD, ROWS), F32)
        for j in range(8):
            if i < 7:
                top = score(i + 1, j, top)
            p = jnp.exp2(s_tile[i % 2, span(j), :] - row_shift)
            total = total + fold(p, jnp.sum)
            p = p.astype(BF16)
            powers[span(j), span(i)] = p
            if i >= EARLY:
                weighted = weighted + dot(vt[:, span(j)], p, 1, 0)
        row_total = jnp.sum(total, axis=0, keepdims=True)
        if i < EARLY:
            sums[i] = row_total
        else:
            give(i, weighted, row_total)

    def part_copy(s):
        return remote(part.at[s], part_in.at[s], PA, s, t_to(s))

    for s in (1, 2, 3):
        w_copy(s).wait_recv()
        part[s] = dot(og[...], wg[s], 1, 0).astype(BF16)
        part_copy(s).start()
    for e in range(8):
        kt[:, span(e)] = kg[span(e), :].astype(F32).T.astype(BF16)
    for s in (1, 2, 3):
        part_copy(s).wait_recv()
        g_sum = g_sum + part_in[s].astype(F32)
    g_own = g_sum.T.astype(BF16)
    gt[0] = g_own

    def g_copy(i):
        source = {5: 3, 7: 3, 6: 4}.get(i, 0)
        target = {5: 1, 7: 3, 6: 2}.get(i, i)
        return remote(gt.at[source], gt.at[i], G, i, z_to(target))

    for i in (3, 4, 1, 2):
        g_copy(i).start()
    for e in near:
        x_copy(e).wait_recv()
    for half in range(2):
        x_pass(half).start()

    for i in range(1, 8):
        l_copy(i).wait_recv()
    log_parts = [l_send[0][0:1, :]] + [l_in[i][0:1, :] for i in range(1, 8)]
    highest = log_parts[0]
    for value in log_parts[1:]:
        highest = jnp.maximum(highest, value)
    factors = [jnp.exp2(value - highest) for value in log_parts]
    total = factors[0]
    for value in factors[1:]:
        total = total + value
    joined = (factors[0] / total) * o_send[0].astype(F32)
    for i in range(1, 8):
        o_copy(i).wait_recv()
        joined = joined + (factors[i] / total) * o_in[i].astype(F32)
    attended = joined.astype(BF16)
    att[span(0, HD), span(0)] = attended

    log_total = highest + jnp.log2(total)
    row_delta = jnp.sum(attended.astype(F32) * g_own.astype(F32), axis=0, keepdims=True)
    upper = lax.broadcasted_iota(jnp.int32, (8, ROWS), 0) < 4
    st_send[...] = jnp.where(upper, log_total, row_delta)
    st_in[0] = st_send[...]

    def st_copy(i):
        return remote(st_send, st_in.at[i], ST, i, z_to(i))

    for i in range(1, 8):
        st_copy(i).start()

    def a_copy(e):
        own = att.at[span(0, HD), span(0)]
        return remote(own, att.at[span(0, HD), span(e)], AT, e, u_to(e))

    def a_pass():
        return remote(att.at[span(0, HD)], att.at[span(1, HD)], AC, 0, t_to(1))

    for e in near:
        a_copy(e).start()
    g_copy(3).wait_recv()
    g_copy(5).start()
    g_copy(7).start()
    g_copy(4).wait_recv()
    g_copy(6).start()

    def dq_copy(i):
        return remote(dq_send.at[i], dq_in.at[i], DQ, i, z_back(i))

    def weigh(i):
        if i:
            if 3 != i != 4:
                g_copy(i).wait_recv()
            st_copy(i).wait_recv()
        factor = jnp.exp2(shift[i] - st_in[i, 0:1, :])
        sums[i] = factor * st_in[i, 4:5, :]
        gs[:, span(i)] = (gt[i].astype(F32) * factor).astype(BF16)

    def query_side(i):
        delta = sums[i]
        g_block = gs[:, span(i)]
        query_sum = jnp.zeros((HD, ROWS), F32)
        for j in range(8):
            prob = dot(vg[span(j), :], g_block, 1, 0)
            slope = ((prob - delta) * powers[span(j), span(i)].astype(F32)).astype(BF16)
            grads[span(j), span(i)] = slope
            query_sum = query_sum + dot(kt[:, span(j)], slope, 1, 0)
        dq_send[i] = query_sum.astype(BF16)
        if i:
            dq_copy(i).start()

    def dk_copy(e):
        return remote(dk_send.at[e], dk_in.at[e], DK, e, u_back(e))

    def dv_copy(e):
        return remote(dv_send.at[e], dv_in.at[e], DV, e, u_back(e))

    for i in (1, 2, 0, 3):
        weigh(i)
        query_side(i)
    for i in range(4, 8):
        weigh(i)
    for e in (6, 2, 7, 5, 4, 3, 1, 0):
        dv_send[e] = dot(powers[span(e), :], gs[...], 1, 1).astype(BF16)
        if e:
            dv_copy(e).start()
    for e in near:
        a_copy(e).wait_recv()
    a_pass().start()
    for i in (7, 5, 6, 4):
        query_side(i)

    self_served = jnp.logical_and(
        jnp.logical_and(co == lax.div(y, 2), xh == lax.rem(y, 2)), y == 2 * xl
    )

    def p_copy(n):
        target = {
            "tensor_1": lax.rem(co + n % 2, 2),
            "context_0": lax.rem(xh + n // 4, 2),
            "context_1": 2 * co + lax.rem(xl + n // 4, 2),
            "context_2": 2 * pair(y, lax.rem(xh + n // 4, 2)) + n // 2 % 2,
        }
        return remote(p_send.at[n], p_in.at[z], S2, n, target, z)

    def p_own(n):
        if n % 2:
            return False
        same = jnp.logical_and(lax.rem(xh + n // 4, 2) == xl, lax.rem(z, 2) == n // 2 % 2)
        return jnp.logical_and(self_served, same)

    for half in range(2):
        x_pass(half).wait_recv()
    a_pass().wait_recv()
    for t in range(2):
        product = dot(xg[t], att[...], 1, 1).astype(BF16)
        for r in range(2):
            for c in range(2):
                n = 4 * t + 2 * r + c
                p_send[n] = product[span(r, PIECE), span(c, HD)]
                if c:
                    p_copy(n).start()
                else:
                    @pl.when(jnp.logical_not(p_own(n)))
                    def _(n=n):
                        p_copy(n).start()

                    @pl.when(p_own(n))
                    def _(n=n):
                        p_in[z] = p_send[n]

    for e in (6, 2, 7, 5, 4, 3, 1, 0):
        dk_send[e] = dot(grads[span(e), :], qg[...], 1, 0).astype(BF16)
        if e:
            dk_copy(e).start()

    total = dv_send[0].astype(F32)
    for e in range(1, 8):
        dv_copy(e).wait_recv()
        total = total + dv_in[e].astype(F32)
    dv_out[...] = total.astype(BF16)
    total = dq_send[0].astype(F32)
    for i in range(1, 8):
        dq_copy(i).wait_recv()
        total = total + dq_in[i].astype(F32)
    dq_out[...] = (total * SCALING).T.astype(BF16)
    for n in range(8):
        @pl.when(jnp.logical_not(jnp.logical_and(self_served, z == n)))
        def _(n=n):
            remote(p_send.at[n], p_in.at[n], S2, n, z_to(1)).wait_recv()

    total = p_in[0].astype(F32)
    for n in range(1, 8):
        total = total + p_in[n].astype(F32)
    dw_out[...] = total
    total = dk_send[0].astype(F32)
    for e in range(1, 8):
        dk_copy(e).wait_recv()
        total = total + dk_in[e].astype(F32)
    dk_out[...] = (total * SCALING).astype(BF16)

    for i in range(1, 8):
        for copy in (q_copy, k_copy, v_copy, g_copy, o_copy, l_copy, st_copy, dq_copy, dk_copy,
                     dv_copy):
            copy(i).wait_send()
        x_copy(i).wait_send()
        a_copy(i).wait_send()
    a_pass().wait_send()
    for half in range(2):
        x_pass(half).wait_send()
    for s in range(1, 4):
        w_copy(s).wait_send()
        part_copy(s).wait_send()
    for n in range(8):
        if n % 2:
            p_copy(n).wait_send()
        else:
            @pl.when(jnp.logical_not(p_own(n)))
            def _(n=n):
                p_copy(n).wait_send()


def hand_over(*refs):
    for source, target in zip(refs[:4], refs[4:]):
        target[...] = source[...]


def local(q, k, v, og, w):
    anywhere = pl.BlockSpec(memory_space=pl.ANY)
    vmem = pl.BlockSpec(memory_space=pltpu.VMEM)
    tokens = 8 * ROWS
    block = (8, ROWS, HD)
    turned = (8, HD, ROWS)
    shapes = (
        jax.ShapeDtypeStruct((ROWS, HD), BF16),
        jax.ShapeDtypeStruct((ROWS, HD), BF16),
        jax.ShapeDtypeStruct((ROWS, HD), BF16),
        jax.ShapeDtypeStruct((PIECE, HD), F32),
    )
    results = pl.pallas_call(
        kernel,
        out_shape=shapes,
        in_specs=[anywhere] * 5,
        out_specs=(vmem,) * 4,
        scratch_shapes=[
            pltpu.VMEM((tokens, HD), BF16),
            pltpu.VMEM((tokens, HD), BF16),
            pltpu.VMEM((tokens, HD), BF16),
            pltpu.VMEM((HD, tokens), BF16),
            pltpu.VMEM((HD, tokens), BF16),
            pltpu.VMEM((ROWS, FEATURES), BF16),
            pltpu.VMEM((FEATURES, ROWS), BF16),
            pltpu.VMEM((4, FEATURES, HD), BF16),
            pltpu.VMEM((4, ROWS, HD), BF16),
            pltpu.VMEM((4, ROWS, HD), BF16),
            pltpu.VMEM(turned, BF16),
            pltpu.VMEM((HD, tokens), BF16),
            pltpu.VMEM((2, tokens, ROWS), F32),
            pltpu.VMEM((tokens, tokens), BF16),
            pltpu.VMEM((tokens, tokens), BF16),
            pltpu.VMEM((8, 1, ROWS), F32),
            pltpu.VMEM((8, 1, ROWS), F32),
            pltpu.VMEM(turned, BF16),
            pltpu.VMEM(turned, BF16),
            pltpu.VMEM((8, 8, ROWS), F32),
            pltpu.VMEM((8, 8, ROWS), F32),
            pltpu.VMEM((8, ROWS), F32),
            pltpu.VMEM((8, 8, ROWS), F32),
            pltpu.VMEM((2, SUBSET, tokens), BF16),
            pltpu.VMEM((2 * HD, tokens), BF16),
            pltpu.VMEM(turned, BF16),
            pltpu.VMEM(turned, BF16),
            pltpu.VMEM(block, BF16),
            pltpu.VMEM(block, BF16),
            pltpu.VMEM(block, BF16),
            pltpu.VMEM(block, BF16),
            pltpu.VMEM((8, PIECE, HD), BF16),
            pltpu.VMEM((8, PIECE, HD), BF16),
            pltpu.SemaphoreType.DMA((17, 8)),
            pltpu.SemaphoreType.DMA((17, 8)),
            pltpu.SemaphoreType.DMA((5,)),
        ],
        compiler_params=pltpu.CompilerParams(
            collective_id=0,
            has_side_effects=True,
            vmem_limit_bytes=56 * 1024 * 1024,
        ),
    )(q, k, v, og, w)
    return pl.pallas_call(
        hand_over,
        out_shape=shapes,
        in_specs=[vmem] * 4,
        out_specs=(vmem,) * 4,
    )(*results)


def solution(mesh):
    torus = Mesh(mesh.devices.reshape(2, 2, 2, 4, 8), TENSOR + CONTEXT)
    tiles = P(CONTEXT, TENSOR)
    return jax.shard_map(
        local,
        mesh=torus,
        in_specs=(tiles, tiles, tiles, tiles, P(None, TENSOR)),
        out_specs=(tiles, tiles, tiles, tiles),
        check_vma=False,
    )
```
